32 devices in a mesh: gx: 4 (over z), gy: 8 (over y, x, core).
Axes of the slice: x: 2, y: 2, z: 4, core: 2. Of those that a mesh axis runs over, the one named last changes fastest.
Arguments:
- right_side: float32 [512, 2048], P('gx', 'gy'), may hold values from -1.2 to 1.2
- shift: float32 [512, 2048], P('gx', 'gy'), may hold values from 0.0001 to 0.004
Outputs:
- solution: float32 [512, 2048], P('gx', 'gy')
- residual: float32 [512, 2048], P('gx', 'gy')
The draws below stay inside these ranges and needn't reach their ends.
All inputs are finite; a program needn't handle non-finite values.
Results may differ from the reference program's by a relative error of at most 0.0003.
Values sent between devices are 32-bit elements; how exact they have to be, the bound alone decides.
A program may use at most 128 MiB of HBM per device.

```python
import math
import jax
import jax.numpy as jnp

LEVELS = 4
COARSE_SWEEPS = 6
NX = 512
NY = 2048


def draw_right_side(key, part):
    return jnp.clip(0.2 * jax.random.normal(key, (NX, NY), jnp.float32), -1.2, 1.2)


def steps_of(own_key, shape, shards, smallest, largest):
    def one(position, shards_of):
        draws = jax.random.uniform(jax.random.fold_in(jax.random.fold_in(own_key, 6), position), (shards_of,), jnp.float32, smallest / len(shards), largest / len(shards))
        return jnp.repeat(jnp.exp(draws), shape[position] // shards_of).reshape((-1,) + (1,) * (len(shape) - position - 1))

    factor_of = one(*shards[0])
    for cut in shards[1:]:
        factor_of = factor_of * one(*cut)
    return factor_of


def setup_inputs(seed: int = 0) -> dict:
    key_list = jax.random.split(jax.random.key(seed), 3)
    right_side = draw_right_side(jax.random.fold_in(key_list[2], 71), 0)
    shift = jnp.clip(jnp.exp(math.log(0.004) - 3.6888795 * jax.random.uniform(key_list[1], (NX, NY), jnp.float32) ** steps_of(key_list[1], (NX, NY), ((0, 4), (1, 8)), -0.2, 0.2)), 0.0001, 0.004)
    return dict(right_side=right_side, shift=shift)


damping = 0.8


def restrict(values):
    rows, columns = values.shape
    blocks = values.reshape(rows // 2, 2, columns // 2, 2)
    return 0.25 * (blocks[:, 0, :, 0] + blocks[:, 1, :, 0] + blocks[:, 0, :, 1] + blocks[:, 1, :, 1])


def prolong(values):
    rows, columns = values.shape
    copies = jnp.broadcast_to(values[:, None, :, None], (rows, 2, columns, 2))
    return copies.reshape(2 * rows, 2 * columns)


def operate_padded(padded, shifts, level):
    centre = padded[1:-1, 1:-1]
    beside = padded[2:, 1:-1] + padded[:-2, 1:-1] + padded[1:-1, 2:] + padded[1:-1, :-2]
    return 4.0 ** (-level) * (4.0 * centre - beside) + shifts * centre


def apply_operator(field, shifts, level):
    return operate_padded(jnp.pad(field, 1), shifts, level)


def sweeps(iterate, source, shifts, level, count):
    diagonal = 4.0 ** (1 - level) + shifts
    for turn in range(count):
        if iterate is None:
            iterate = damping * source / diagonal
        else:
            iterate = iterate + damping * (source - apply_operator(iterate, shifts, level)) / diagonal
    return iterate


def coarse_solve(iterate, source, shifts):
    unit_total = jnp.sum(apply_operator(jnp.ones_like(source), shifts, LEVELS))
    if iterate is None:
        left = jnp.sum(source)
        iterate = jnp.zeros_like(source) + left / unit_total
    else:
        left = jnp.sum(source - apply_operator(iterate, shifts, LEVELS))
        iterate = iterate + left / unit_total
    return sweeps(iterate, source, shifts, LEVELS, COARSE_SWEEPS)


def vcycle(level, iterate, source, shift_list):
    shifts = shift_list[level]
    if level == LEVELS:
        return coarse_solve(iterate, source, shifts)
    iterate = sweeps(iterate, source, shifts, level, 2)
    coarse_rhs = restrict(source - apply_operator(iterate, shifts, level))
    iterate = iterate + prolong(vcycle(level + 1, None, coarse_rhs, shift_list))
    return sweeps(iterate, source, shifts, level, 2)


def fcycle(level, source, shift_list):
    shifts = shift_list[level]
    if level == LEVELS:
        return coarse_solve(None, source, shifts)
    iterate = sweeps(None, source, shifts, level, 2)
    coarse_rhs = restrict(source - apply_operator(iterate, shifts, level))
    correction = fcycle(level + 1, coarse_rhs, shift_list)
    correction = vcycle(level + 1, correction, coarse_rhs, shift_list)
    iterate = iterate + prolong(correction)
    return sweeps(iterate, source, shifts, level, 2)


def reference(right_side, shift):
    shift_list = [shift]
    for level in range(LEVELS):
        shift_list.append(restrict(shift_list[-1]))
    solution = fcycle(0, right_side, shift_list)
    residual = right_side - apply_operator(solution, shift, 0)
    return solution, residual
```

```python
import functools

import jax
import jax.numpy as jnp
from jax import lax
from jax.experimental import pallas as pl
from jax.experimental.pallas import tpu as pltpu
from jax.sharding import PartitionSpec as P

COARSE_SWEEPS = 6
DAMPING = 0.8
MESH = pl.DeviceIdType.MESH
F32 = jnp.float32
BF16 = jnp.bfloat16

ROWS_PAD = 8
HALO = 24


def iota(shape, dim):
    return lax.broadcasted_iota(jnp.int32, shape, dim)


def put_strips(ref, at, values):
    for k in range(ref.shape[0]):
        ref[k, at, :] = values[:, k * 128 : (k + 1) * 128]


def get_strips(ref, at, count=None):
    return jnp.concatenate([ref[k, at, :] for k in range(count or ref.shape[0])], 1)


def exact_dot(values, selector):
    first = values.astype(BF16)
    rest = values - first.astype(F32)
    second = rest.astype(BF16)
    third = (rest - second.astype(F32)).astype(BF16)
    dot = functools.partial(jnp.dot, preferred_element_type=F32)
    return dot(first, selector) + (dot(second, selector) + dot(third, selector))


def kernel(
    gx_count, gy_count, g_ref, s_ref, sol_ref, res_ref,
    gE, sE, wE, vA, vB, fine_add,
    g1, s1, w1, a1, b1, r1,
    send_l, send_r, recv_l, recv_r,
    down0, up0, down1, spread,
    rbuf, s2, w2, g2, a2, b2, s3, w3, g3, a3, b3, s4, w4, g4, a4, b4, picked,
    halo_send, halo_recv, all_send, all_recv,
):
    gx, gy = lax.axis_index("gx"), lax.axis_index("gy")
    total = gx_count * gy_count
    me = gx * gy_count + gy
    rows, cols = g_ref.shape
    base = ROWS_PAD + HALO
    base1 = ROWS_PAD + (ROWS_PAD + HALO) // 2
    ext, width = gE.shape
    ext1, width1 = ext // 2, g1.shape[1]
    lanes = 128

    zero_halo = jnp.zeros((base, width), F32)
    for ref in (gE, sE):
        ref[0:base, :] = zero_halo
        ref[base + rows : ext, :] = zero_halo
    for ref in (recv_l, recv_r):
        ref[...] = jnp.zeros(ref.shape, F32)
    barrier = pltpu.get_barrier_semaphore()

    @pl.loop(1, total)
    def _(k):
        peer = lax.rem(me + k, total)
        pl.semaphore_signal(
            barrier, inc=1, device_id=(peer // gy_count, lax.rem(peer, gy_count)), device_id_type=MESH
        )

    lane = iota((rows, lanes), 1)
    half = lanes // 2
    send_l[...] = jnp.where(lane < half, g_ref[:, 0:lanes], pltpu.roll(s_ref[:, 0:lanes], half, 1))
    send_r[...] = jnp.where(
        lane < half, pltpu.roll(s_ref[:, cols - lanes : cols], half, 1), g_ref[:, cols - lanes : cols]
    )

    l0 = iota((width, width1), 0)
    col0 = jnp.where(l0 < cols + half, l0, l0 - width)
    down0[...] = jnp.where(
        ((col0 + 2 * width1) // 2) % width1 == iota((width, width1), 1), 1.0, 0.0
    ).astype(BF16)
    l0 = iota((width1, width), 1)
    col0 = jnp.where(l0 < cols + half, l0, l0 - width)
    up0[...] = jnp.where(
        ((col0 + 2 * width1) // 2) % width1 == iota((width1, width), 0), 1.0, 0.0
    ).astype(BF16)
    l1 = iota((width1, lanes), 0)
    j2 = l1 // 2
    place = (j2 % 4) * 16 + j2 // 4
    down1[...] = jnp.where(
        (l1 < lanes) & (iota((width1, lanes), 1) % half == place), 1.0, 0.0
    ).astype(BF16)
    q_count = s2.shape[2]
    p_count = s2.shape[1]
    m1 = iota((q_count, width1), 1)
    col1 = jnp.where(m1 < lanes + half // 2, m1, m1 - width1)
    wide = gy * half + (col1 + 512) // 2 - 256
    for r in range(4):
        spread[r * q_count : (r + 1) * q_count, :] = jnp.where(
            wide == 4 * iota((q_count, width1), 0) + r, 1.0, 0.0
        ).astype(BF16)

    def pack_level2(source):
        parts = []
        for t in range(4):
            start = base1 + 2 * t
            parts.append(
                get_strips(source, pl.ds(start, 8, 8)) + get_strips(source, pl.ds(start + 1, 8, 8))
            )
        means = 0.25 * exact_dot(jnp.concatenate(parts, 0), down1[...])
        low = iota((16, lanes), 1) < half
        return jnp.where(low, means[0:16], means[16:32])

    half_rows = rows // 2
    own_strips = cols // lanes
    for k in range(own_strips):
        fine_add[k, base : base + rows, :] = s_ref[:, k * lanes : (k + 1) * lanes]
    own = get_strips(fine_add, pl.ds(base, half_rows, 2), own_strips)
    own = own + get_strips(fine_add, pl.ds(base + 1, half_rows, 2), own_strips)
    put_strips(r1, slice(base1, base1 + half_rows), 0.25 * exact_dot(own, down0[0:cols, :]))
    rbuf[0, me] = pack_level2(r1)
    gE[base : base + rows, 0:cols] = g_ref[...]
    sE[base : base + rows, 0:cols] = s_ref[...]

    pl.semaphore_wait(barrier, total - 1)

    top, bottom = slice(0, HALO), slice(rows - HALO, rows)
    above, below = slice(ROWS_PAD, base), slice(base + rows, base + rows + HALO)
    middle = slice(base, base + rows)
    sends = (
        (0, -1, send_l, recv_r.at[middle, :]),
        (0, 1, send_r, recv_l.at[middle, :]),
        (-1, -1, send_l.at[top, :], recv_r.at[below, :]),
        (1, -1, send_l.at[bottom, :], recv_r.at[above, :]),
        (-1, 1, send_r.at[top, :], recv_l.at[below, :]),
        (1, 1, send_r.at[bottom, :], recv_l.at[above, :]),
        (-1, 0, g_ref.at[top, :], gE.at[below, 0:cols]),
        (-1, 0, s_ref.at[top, :], sE.at[below, 0:cols]),
        (1, 0, g_ref.at[bottom, :], gE.at[above, 0:cols]),
        (1, 0, s_ref.at[bottom, :], sE.at[above, 0:cols]),
    )

    def inside(dx, dy):
        ok = None
        for step, at, count in ((dx, gx, gx_count), (dy, gy, gy_count)):
            if step:
                here = (at > 0) if step < 0 else (at < count - 1)
                ok = here if ok is None else ok & here
        return ok

    def halo_copy(n, dx, dy, source, target):
        return pltpu.make_async_remote_copy(
            src_ref=source, dst_ref=target, send_sem=halo_send.at[n], recv_sem=halo_recv.at[n],
            device_id=(gx + dx, gy + dy), device_id_type=MESH,
        )

    for n, (dx, dy, source, target) in enumerate(sends):
        @pl.when(inside(dx, dy))
        def _():
            halo_copy(n, dx, dy, source, target).start()

    def block_copy(turn, k, slot, peer):
        return pltpu.make_async_remote_copy(
            src_ref=rbuf.at[turn, me], dst_ref=rbuf.at[turn, slot],
            send_sem=all_send.at[turn, k], recv_sem=all_recv.at[turn, slot],
            device_id=(peer // gy_count, lax.rem(peer, gy_count)), device_id_type=MESH,
        )

    def gather_start(turn):
        @pl.loop(1, total)
        def _(k):
            block_copy(turn, k, me, lax.rem(me + k, total)).start()

    def gather_wait(turn):
        @pl.loop(1, total)
        def _(k):
            other = lax.rem(me + total - k, total)
            block_copy(turn, k, other, other).wait_recv()

    def gather_sent(turn):
        @pl.loop(1, total)
        def _(k):
            block_copy(turn, k, me, lax.rem(me + k, total)).wait_send()

    gather_start(0)
    zero_tile = jnp.zeros((ROWS_PAD, width), F32)
    for ref in (vA, vB):
        ref[0:ROWS_PAD, :] = zero_tile
        ref[ext - ROWS_PAD : ext, :] = zero_tile
    for ref in (a1, b1, g1):
        ref[0:ROWS_PAD, :] = jnp.zeros((ROWS_PAD, width1), F32)
        ref[ROWS_PAD + ext1 : 2 * ROWS_PAD + ext1, :] = jnp.zeros((ROWS_PAD, width1), F32)
    for ref in (a2, b2, a3, b3, a4, b4):
        for i in range(ref.shape[0]):
            ref[i, 0:8, :] = jnp.zeros((8, q_count), F32)
            ref[i, 8 + p_count : 16 + p_count, :] = jnp.zeros((8, q_count), F32)

    for n, (dx, dy, source, target) in enumerate(sends):
        @pl.when(inside(-dx, -dy))
        def _():
            halo_copy(n, -dx, -dy, source, target).wait_recv()

    lane_e = iota((ext, lanes), 1)
    gE[:, cols:width] = jnp.where(lane_e < half, recv_r[...], recv_l[...])
    sE[:, cols:width] = pltpu.roll(jnp.where(lane_e < half, recv_l[...], recv_r[...]), half, 1)

    def weight(shifts, first_row, own_rows, own_cols, split, level):
        shape = shifts.shape
        at_row = gx * own_rows + iota(shape, 0) + first_row
        lane_at = iota(shape, 1)
        at_col = gy * own_cols + jnp.where(lane_at < own_cols + split, lane_at, lane_at - shape[1])
        good = (at_row >= 0) & (at_row < gx_count * own_rows)
        good = good & (at_col >= 0) & (at_col < gy_count * own_cols)
        return jnp.where(good, DAMPING / (4.0 ** (1 - level) + shifts), 0.0)

    def around(v, lo, size):
        span = v.shape[1]
        mid = v[lo : lo + size, :]
        beside = pltpu.roll(mid, 1, 1) + pltpu.roll(mid, span - 1, 1)
        return mid, beside + (v[lo - 1 : lo - 1 + size, :] + v[lo + 1 : lo + 1 + size, :])

    def sweep_block(v, out, g, w, level):
        scale = 4.0 ** (-level)
        for lo in range(ROWS_PAD, v.shape[0] - ROWS_PAD, 8):
            mid, beside = around(v, lo, 8)
            at = slice(lo, lo + 8)
            out[at, :] = (1.0 - DAMPING) * mid + w[at, :] * (g[at, :] + scale * beside)

    def residual_block(v, out, g, s, level):
        scale = 4.0 ** (-level)
        for lo in range(ROWS_PAD, v.shape[0] - ROWS_PAD, 8):
            mid, beside = around(v, lo, 8)
            at = slice(lo, lo + 8)
            put_strips(out, at, g[at, :] - (scale * (4.0 * mid - beside) + s[at, :] * mid))

    chunk = 16
    for lo in range(0, ext, chunk):
        at = slice(lo, lo + chunk)
        wE[at, :] = weight(sE[at, :], lo - base, rows, cols, half, 0)
    for lo in range(ROWS_PAD, ext - ROWS_PAD, 8):
        at = slice(lo, lo + 8)
        vA[at, :] = wE[at, :] * gE[at, :]
    sweep_block(vA, vB, gE, wE, 0)
    put_strips(fine_add, slice(0, ROWS_PAD), zero_tile)
    put_strips(fine_add, slice(ext - ROWS_PAD, ext), zero_tile)
    residual_block(vB, fine_add, gE, sE, 0)

    in1 = slice(ROWS_PAD, ROWS_PAD + ext1)

    def halved():
        pairs = get_strips(fine_add, pl.ds(0, ext1, 2)) + get_strips(fine_add, pl.ds(1, ext1, 2))
        return 0.25 * exact_dot(pairs, down0[...])

    g1[in1, :] = halved()
    put_strips(fine_add, slice(0, ext), sE[...])
    s1[in1, :] = halved()
    w1[in1, :] = weight(s1[in1, :], ROWS_PAD - base1, half_rows, cols // 2, half // 2, 1)
    a1[in1, :] = w1[in1, :] * g1[in1, :]
    sweep_block(a1, b1, g1, w1, 1)
    residual_block(b1, r1, g1, s1, 1)
    rbuf[1, me] = pack_level2(r1)
    gather_start(1)

    block = (lane_e[0:8] // 16)

    def unpack(turn, target):
        for x in range(gx_count):
            for u in range(gy_count // 8):
                for tl in range(2):
                    tiles = [rbuf[turn, x * gy_count + u * 8 + g, tl * 8 : tl * 8 + 8, :] for g in range(8)]
                    for bit in (1, 2, 4):
                        keep = (block & bit) == 0
                        fresh = list(tiles)
                        for g in range(8):
                            if g & bit == 0:
                                lo, hi = tiles[g], tiles[g | bit]
                                fresh[g] = jnp.where(keep, lo, pltpu.roll(hi, 16 * bit, 1))
                                fresh[g | bit] = jnp.where(keep, pltpu.roll(lo, lanes - 16 * bit, 1), hi)
                        tiles = fresh
                    for b in range(8):
                        t, r = (b // 4) * 2 + tl, b % 4
                        target[t * 4 + r, 8 * x : 8 * x + 8, u * lanes : (u + 1) * lanes] = tiles[b]

    lane_q = iota((p_count, q_count), 1)
    rows_q = slice(8, 8 + p_count)

    def sides(v, n, t, r):
        mid = v[t * n + r, rows_q, :]
        if t > 0:
            north = v[(t - 1) * n + r, rows_q, :]
        else:
            north = v[(n - 1) * n + r, 7 : 7 + p_count, :]
        if t < n - 1:
            south = v[(t + 1) * n + r, rows_q, :]
        else:
            south = v[r, 9 : 9 + p_count, :]
        if r > 0:
            west = v[t * n + r - 1, rows_q, :]
        else:
            west = jnp.where(lane_q == 0, 0.0, pltpu.roll(v[t * n + n - 1, rows_q, :], 1, 1))
        if r < n - 1:
            east = v[t * n + r + 1, rows_q, :]
        else:
            east = jnp.where(
                lane_q == q_count - 1, 0.0, pltpu.roll(v[t * n, rows_q, :], q_count - 1, 1)
            )
        return mid, (north + south) + (west + east)

    level_refs = {2: (s2, w2, g2, a2, b2, 4), 3: (s3, w3, g3, a3, b3, 2), 4: (s4, w4, g4, a4, b4, 1)}

    def sweep(level, v, out):
        s, w, g, _, _, n = level_refs[level]
        for t in range(n):
            for r in range(n):
                i = t * n + r
                mid, beside = sides(v, n, t, r)
                out[i, rows_q, :] = (1.0 - DAMPING) * mid + w[i] * (g[i] + 4.0 ** (-level) * beside)

    def first_sweep(level, out):
        s, w, g, _, _, n = level_refs[level]
        for i in range(n * n):
            out[i, rows_q, :] = w[i] * g[i]

    def restricted(level, v):
        s, w, g, _, _, n = level_refs[level]
        coarse_g = level_refs[level + 1][2]
        for t in range(n // 2):
            for r in range(n // 2):
                sums = None
                for dt in range(2):
                    for dr in range(2):
                        i = (2 * t + dt) * n + 2 * r + dr
                        mid, beside = sides(v, n, 2 * t + dt, 2 * r + dr)
                        left = g[i] - (4.0 ** (-level) * (4.0 * mid - beside) + s[i] * mid)
                        sums = left if sums is None else sums + left
                coarse_g[t * (n // 2) + r] = 0.25 * sums

    def correct(level, v, e):
        n = level_refs[level][5]
        for t in range(n):
            for r in range(n):
                i = t * n + r
                v[i, rows_q, :] = v[i, rows_q, :] + e[(t // 2) * (n // 2) + r // 2, rows_q, :]

    def prepare(level):
        s, w, _, _, _, n = level_refs[level]
        for i in range(n * n):
            w[i] = DAMPING / (4.0 ** (1 - level) + s[i])
        if level < 4:
            coarse_s = level_refs[level + 1][0]
            m = n // 2
            for t in range(m):
                for r in range(m):
                    i = 2 * t * n + 2 * r
                    coarse_s[t * m + r] = 0.25 * ((s[i] + s[i + n]) + (s[i + 1] + s[i + n + 1]))

    def total_of(x):
        return jnp.sum(jnp.sum(x, axis=0, keepdims=True), axis=1, keepdims=True)

    gather_wait(0)
    unpack(0, s2)
    for level in (2, 3, 4):
        prepare(level)
    row_q = iota((p_count, q_count), 0)
    edges = jnp.where(row_q == 0, 1.0, 0.0) + jnp.where(row_q == p_count - 1, 1.0, 0.0)
    edges = edges + jnp.where(lane_q == 0, 1.0, 0.0) + jnp.where(lane_q == q_count - 1, 1.0, 0.0)
    per_unit = 1.0 / total_of(4.0 ** (-4) * edges + s4[0])

    def coarse(v, from_zero):
        if from_zero:
            shifted = jnp.zeros((p_count, q_count), F32) + total_of(g4[0]) * per_unit
        else:
            mid, beside = sides(v, 1, 0, 0)
            left = g4[0] - (4.0 ** (-4) * (4.0 * mid - beside) + s4[0] * mid)
            shifted = mid + total_of(left) * per_unit
        now, later = a4, b4
        now[0, rows_q, :] = shifted
        for _ in range(COARSE_SWEEPS):
            sweep(4, now, later)
            now, later = later, now
        return now

    def vcycle(level, v):
        if level == 4:
            return coarse(v, v is None)
        _, _, _, a, b, n = level_refs[level]
        if v is None:
            first_sweep(level, a)
            sweep(level, a, b)
            now, later = b, a
        else:
            later = b if v is a else a
            sweep(level, v, later)
            sweep(level, later, v)
            now = v
        restricted(level, now)
        correct(level, now, vcycle(level + 1, None))
        sweep(level, now, later)
        sweep(level, later, now)
        return now

    def fcycle(level):
        if level == 4:
            return coarse(None, True)
        _, _, _, a, b, n = level_refs[level]
        first_sweep(level, a)
        sweep(level, a, b)
        restricted(level, b)
        e = fcycle(level + 1)
        e = vcycle(level + 1, e)
        correct(level, b, e)
        sweep(level, b, a)
        sweep(level, a, b)
        return b

    def add_level2(e, v):
        for t in range(4):
            tiles = [e[t * 4 + r, pl.ds(pl.multiple_of(gx * 8, 8), 24), :] for r in range(4)]
            picked[t] = exact_dot(jnp.concatenate(tiles, 1), spread[...])
        for t in range(4):
            for a in range(2):
                at = pl.ds(ROWS_PAD + 2 * t + a, ext1 // 8, 8)
                put_strips(r1, at, picked[t, 6 : 6 + ext1 // 8, :])
        v[in1, :] = v[in1, :] + get_strips(r1, in1)

    gather_wait(1)
    unpack(1, g2)
    e = fcycle(2)
    e = vcycle(2, e)
    add_level2(e, b1)
    sweep_block(b1, a1, g1, w1, 1)
    sweep_block(a1, b1, g1, w1, 1)
    sweep_block(b1, a1, g1, w1, 1)
    sweep_block(a1, b1, g1, w1, 1)
    residual_block(b1, r1, g1, s1, 1)
    rbuf[2, me] = pack_level2(r1)
    gather_start(2)
    gather_wait(2)
    unpack(2, g2)
    add_level2(vcycle(2, None), b1)
    sweep_block(b1, a1, g1, w1, 1)
    sweep_block(a1, b1, g1, w1, 1)
    raised = exact_dot(b1[in1, :], up0[...])
    put_strips(fine_add, pl.ds(0, ext1, 2), raised)
    put_strips(fine_add, pl.ds(1, ext1, 2), raised)
    for lo in range(ROWS_PAD, ext - ROWS_PAD, 8):
        at = slice(lo, lo + 8)
        vB[at, :] = vB[at, :] + get_strips(fine_add, at)
    sweep_block(vB, vA, gE, wE, 0)
    sweep_block(vA, vB, gE, wE, 0)
    for lo in range(0, rows, 8):
        mid, beside = around(vB, base + lo, 8)
        at = slice(base + lo, base + lo + 8)
        left = gE[at, :] - ((4.0 * mid - beside) + sE[at, :] * mid)
        sol_ref[lo : lo + 8, :] = mid[:, 0:cols]
        res_ref[lo : lo + 8, :] = left[:, 0:cols]

    for n, (dx, dy, source, target) in enumerate(sends):
        @pl.when(inside(dx, dy))
        def _():
            halo_copy(n, dx, dy, source, target).wait_send()
    for turn in range(3):
        gather_sent(turn)


def solution(mesh):
    gx_count, gy_count = mesh.shape["gx"], mesh.shape["gy"]
    total = gx_count * gy_count

    def body(right_side, shift):
        rows, cols = right_side.shape
        assert cols == 256 and rows % 64 == 0 and gy_count % 8 == 0
        ext, width = rows + 2 * (HALO + ROWS_PAD), cols + 128
        ext1, width1 = ext // 2 + 2 * ROWS_PAD, 256
        p, q = rows // 16 * gx_count, cols // 16 * gy_count
        V = pltpu.VMEM
        big = [V((ext, width), F32)] * 5 + [V((width // 128, ext, 128), F32)]
        one = [V((ext1, width1), F32)] * 5 + [V((width1 // 128, ext1, 128), F32)]
        levels = []
        for n in (16, 4, 1):
            levels += [V((n, p, q), F32)] * 3 + [V((n, p + 16, q), F32)] * 2
        scratch = (
            big + one
            + [V((rows, 128), F32)] * 2 + [V((ext, 128), F32)] * 2
            + [V((width, width1), BF16), V((width1, width), BF16), V((width1, 128), BF16), V((4 * q, width1), BF16)]
            + [V((3, total, 16, 128), F32)]
            + levels
            + [V((4, 24, width1), F32)]
            + [
                pltpu.SemaphoreType.DMA((10,)), pltpu.SemaphoreType.DMA((10,)),
                pltpu.SemaphoreType.DMA((3, total)), pltpu.SemaphoreType.DMA((3, total)),
            ]
        )
        out = jax.ShapeDtypeStruct(right_side.shape, F32)
        return pl.pallas_call(
            functools.partial(kernel, gx_count, gy_count),
            out_shape=(out, out),
            in_specs=[pl.BlockSpec(memory_space=pltpu.VMEM)] * 2,
            out_specs=(pl.BlockSpec(memory_space=pltpu.VMEM),) * 2,
            scratch_shapes=scratch,
            compiler_params=pltpu.CompilerParams(
                collective_id=0, has_side_effects=True, vmem_limit_bytes=60 * 1024 * 1024
            ),
        )(right_side, shift)

    spec = P("gx", "gy")
    return jax.shard_map(body, mesh=mesh, in_specs=(spec, spec), out_specs=(spec, spec), check_vma=False)
```

```python
import functools

import jax
import jax.numpy as jnp
from jax import lax
from jax.experimental import pallas as pl
from jax.experimental.pallas import tpu as pltpu
from jax.sharding import PartitionSpec as P

COARSE_SWEEPS = 6
DAMPING = 0.8
MESH = pl.DeviceIdType.MESH
F32 = jnp.float32
BF16 = jnp.bfloat16

ROWS_PAD = 8
HALO = 24


def iota(shape, dim):
    return lax.broadcasted_iota(jnp.int32, shape, dim)


def put_strips(ref, at, values):
    for k in range(ref.shape[0]):
        ref[k, at, :] = values[:, k * 128 : (k + 1) * 128]


def get_strips(ref, at, count=None):
    return jnp.concatenate([ref[k, at, :] for k in range(count or ref.shape[0])], 1)


def exact_dot(values, selector):
    first = values.astype(BF16)
    rest = values - first.astype(F32)
    second = rest.astype(BF16)
    third = (rest - second.astype(F32)).astype(BF16)
    dot = functools.partial(jnp.dot, preferred_element_type=F32)
    return dot(first, selector) + (dot(second, selector) + dot(third, selector))


def kernel(
    gx_count, gy_count, g_ref, s_ref, out_ref,
    gE, sE, wE, vA, vB, fine_add,
    g1, s1, w1, a1, b1, r1,
    send_l, send_r, recv_l, recv_r,
    down0, up0, down1, spread,
    rbuf, s2, w2, g2, a2, b2, s3, w3, g3, a3, b3, s4, w4, g4, a4, b4, picked,
    halo_send, halo_recv, all_send, all_recv,
):
    gx, gy = lax.axis_index("gx"), lax.axis_index("gy")
    total = gx_count * gy_count
    me = gx * gy_count + gy
    rows, cols = g_ref.shape
    base = ROWS_PAD + HALO
    base1 = ROWS_PAD + (ROWS_PAD + HALO) // 2
    ext, width = gE.shape
    ext1, width1 = ext // 2, g1.shape[1]
    lanes = 128

    zero_halo = jnp.zeros((base, width), F32)
    for ref in (gE, sE):
        ref[0:base, :] = zero_halo
        ref[base + rows : ext, :] = zero_halo
    for ref in (recv_l, recv_r):
        ref[...] = jnp.zeros(ref.shape, F32)
    barrier = pltpu.get_barrier_semaphore()

    @pl.loop(1, total)
    def _(k):
        peer = lax.rem(me + k, total)
        pl.semaphore_signal(
            barrier, inc=1, device_id=(peer // gy_count, lax.rem(peer, gy_count)), device_id_type=MESH
        )

    lane = iota((rows, lanes), 1)
    half = lanes // 2
    send_l[...] = jnp.where(lane < half, g_ref[:, 0:lanes], pltpu.roll(s_ref[:, 0:lanes], half, 1))
    send_r[...] = jnp.where(
        lane < half, pltpu.roll(s_ref[:, cols - lanes : cols], half, 1), g_ref[:, cols - lanes : cols]
    )

    l0 = iota((width, width1), 0)
    col0 = jnp.where(l0 < cols + half, l0, l0 - width)
    down0[...] = jnp.where(
        ((col0 + 2 * width1) // 2) % width1 == iota((width, width1), 1), 1.0, 0.0
    ).astype(BF16)
    l0 = iota((width1, width), 1)
    col0 = jnp.where(l0 < cols + half, l0, l0 - width)
    up0[...] = jnp.where(
        ((col0 + 2 * width1) // 2) % width1 == iota((width1, width), 0), 1.0, 0.0
    ).astype(BF16)
    l1 = iota((width1, lanes), 0)
    j2 = l1 // 2
    place = (j2 % 4) * 16 + j2 // 4
    down1[...] = jnp.where(
        (l1 < lanes) & (iota((width1, lanes), 1) % half == place), 1.0, 0.0
    ).astype(BF16)
    q_count = s2.shape[2]
    p_count = s2.shape[1]
    m1 = iota((q_count, width1), 1)
    col1 = jnp.where(m1 < lanes + half // 2, m1, m1 - width1)
    wide = gy * half + (col1 + 512) // 2 - 256
    for r in range(4):
        spread[r * q_count : (r + 1) * q_count, :] = jnp.where(
            wide == 4 * iota((q_count, width1), 0) + r, 1.0, 0.0
        ).astype(BF16)

    def pack_level2(source):
        parts = []
        for t in range(4):
            start = base1 + 2 * t
            parts.append(
                get_strips(source, pl.ds(start, 8, 8)) + get_strips(source, pl.ds(start + 1, 8, 8))
            )
        means = 0.25 * exact_dot(jnp.concatenate(parts, 0), down1[...])
        low = iota((16, lanes), 1) < half
        return jnp.where(low, means[0:16], means[16:32])

    half_rows = rows // 2
    own_strips = cols // lanes
    for k in range(own_strips):
        fine_add[k, base : base + rows, :] = s_ref[:, k * lanes : (k + 1) * lanes]
    own = get_strips(fine_add, pl.ds(base, half_rows, 2), own_strips)
    own = own + get_strips(fine_add, pl.ds(base + 1, half_rows, 2), own_strips)
    put_strips(r1, slice(base1, base1 + half_rows), 0.25 * exact_dot(own, down0[0:cols, :]))
    rbuf[0, me] = pack_level2(r1)
    gE[base : base + rows, 0:cols] = g_ref[...]
    sE[base : base + rows, 0:cols] = s_ref[...]

    pl.semaphore_wait(barrier, total - 1)

    top, bottom = slice(0, HALO), slice(rows - HALO, rows)
    above, below = slice(ROWS_PAD, base), slice(base + rows, base + rows + HALO)
    middle = slice(base, base + rows)
    sends = (
        (0, -1, send_l, recv_r.at[middle, :]),
        (0, 1, send_r, recv_l.at[middle, :]),
        (-1, -1, send_l.at[top, :], recv_r.at[below, :]),
        (1, -1, send_l.at[bottom, :], recv_r.at[above, :]),
        (-1, 1, send_r.at[top, :], recv_l.at[below, :]),
        (1, 1, send_r.at[bottom, :], recv_l.at[above, :]),
        (-1, 0, g_ref.at[top, :], gE.at[below, 0:cols]),
        (-1, 0, s_ref.at[top, :], sE.at[below, 0:cols]),
        (1, 0, g_ref.at[bottom, :], gE.at[above, 0:cols]),
        (1, 0, s_ref.at[bottom, :], sE.at[above, 0:cols]),
    )

    def inside(dx, dy):
        ok = None
        for step, at, count in ((dx, gx, gx_count), (dy, gy, gy_count)):
            if step:
                here = (at > 0) if step < 0 else (at < count - 1)
                ok = here if ok is None else ok & here
        return ok

    def halo_copy(n, dx, dy, source, target):
        return pltpu.make_async_remote_copy(
            src_ref=source, dst_ref=target, send_sem=halo_send.at[n], recv_sem=halo_recv.at[n],
            device_id=(gx + dx, gy + dy), device_id_type=MESH,
        )

    for n, (dx, dy, source, target) in enumerate(sends):
        @pl.when(inside(dx, dy))
        def _():
            halo_copy(n, dx, dy, source, target).start()

    core = lax.rem(gy, 2)
    per_row = gy_count // 2
    chips = total // 2
    chip = me // 2
    partner = (gx, gy + 1 - 2 * core)

    def zigzag(j):
        odd = lax.rem(j, 2)
        return odd * ((j + 1) // 2) + (1 - odd) * (chips - j // 2)

    def block_copy(turn, n, slot, peer):
        return pltpu.make_async_remote_copy(
            src_ref=rbuf.at[turn, slot], dst_ref=rbuf.at[turn, slot],
            send_sem=all_send.at[turn, n], recv_sem=all_recv.at[turn, slot],
            device_id=peer, device_id_type=MESH,
        )

    def direct(turn, j):
        other = lax.rem(chip + zigzag(j), chips)
        return block_copy(turn, j, me, (other // per_row, 2 * lax.rem(other, per_row) + core))

    def onward(turn, j):
        slot = 2 * lax.rem(chip + chips - zigzag(j), chips) + core
        return block_copy(turn, chips + j, slot, partner)

    def gather_start(turn):
        block_copy(turn, 0, me, partner).start()

        @pl.loop(1, chips)
        def _(j):
            direct(turn, chips - j).start()

    def gather_wait(turn):
        @pl.loop(1, chips)
        def _(j):
            copy = onward(turn, j)
            copy.wait_recv()
            copy.start()

        block_copy(turn, 0, me + 1 - 2 * core, partner).wait_recv()

        @pl.loop(1, chips)
        def _(j):
            slot = 2 * lax.rem(chip + chips - zigzag(j), chips) + 1 - core
            block_copy(turn, chips + j, slot, partner).wait_recv()

    def gather_sent(turn):
        block_copy(turn, 0, me, partner).wait_send()

        @pl.loop(1, chips)
        def _(j):
            direct(turn, j).wait_send()
            onward(turn, j).wait_send()

    gather_start(0)
    zero_tile = jnp.zeros((ROWS_PAD, width), F32)
    for ref in (vA, vB):
        ref[0:ROWS_PAD, :] = zero_tile
        ref[ext - ROWS_PAD : ext, :] = zero_tile
    for ref in (a1, b1, g1):
        ref[0:ROWS_PAD, :] = jnp.zeros((ROWS_PAD, width1), F32)
        ref[ROWS_PAD + ext1 : 2 * ROWS_PAD + ext1, :] = jnp.zeros((ROWS_PAD, width1), F32)
    for ref in (a2, b2, a3, b3, a4, b4):
        for i in range(ref.shape[0]):
            ref[i, 0:8, :] = jnp.zeros((8, q_count), F32)
            ref[i, 8 + p_count : 16 + p_count, :] = jnp.zeros((8, q_count), F32)

    for n, (dx, dy, source, target) in enumerate(sends):
        @pl.when(inside(-dx, -dy))
        def _():
            halo_copy(n, -dx, -dy, source, target).wait_recv()

    lane_e = iota((ext, lanes), 1)
    gE[:, cols:width] = jnp.where(lane_e < half, recv_r[...], recv_l[...])
    sE[:, cols:width] = pltpu.roll(jnp.where(lane_e < half, recv_l[...], recv_r[...]), half, 1)

    def weight(shifts, first_row, own_rows, own_cols, split, level):
        shape = shifts.shape
        at_row = gx * own_rows + iota(shape, 0) + first_row
        lane_at = iota(shape, 1)
        at_col = gy * own_cols + jnp.where(lane_at < own_cols + split, lane_at, lane_at - shape[1])
        good = (at_row >= 0) & (at_row < gx_count * own_rows)
        good = good & (at_col >= 0) & (at_col < gy_count * own_cols)
        return jnp.where(good, DAMPING / (4.0 ** (1 - level) + shifts), 0.0)

    def around(v, lo, size):
        span = v.shape[1]
        mid = v[lo : lo + size, :]
        beside = pltpu.roll(mid, 1, 1) + pltpu.roll(mid, span - 1, 1)
        return mid, beside + (v[lo - 1 : lo - 1 + size, :] + v[lo + 1 : lo + 1 + size, :])

    def sweep_block(v, out, g, w, level):
        scale = 4.0 ** (-level)
        for lo in range(ROWS_PAD, v.shape[0] - ROWS_PAD, 8):
            mid, beside = around(v, lo, 8)
            at = slice(lo, lo + 8)
            out[at, :] = (1.0 - DAMPING) * mid + w[at, :] * (g[at, :] + scale * beside)

    def residual_block(v, out, g, s, level):
        scale = 4.0 ** (-level)
        for lo in range(ROWS_PAD, v.shape[0] - ROWS_PAD, 8):
            mid, beside = around(v, lo, 8)
            at = slice(lo, lo + 8)
            put_strips(out, at, g[at, :] - (scale * (4.0 * mid - beside) + s[at, :] * mid))

    chunk = 16
    for lo in range(0, ext, chunk):
        at = slice(lo, lo + chunk)
        wE[at, :] = weight(sE[at, :], lo - base, rows, cols, half, 0)
    for lo in range(ROWS_PAD, ext - ROWS_PAD, 8):
        at = slice(lo, lo + 8)
        vA[at, :] = wE[at, :] * gE[at, :]
    sweep_block(vA, vB, gE, wE, 0)
    put_strips(fine_add, slice(0, ROWS_PAD), zero_tile)
    put_strips(fine_add, slice(ext - ROWS_PAD, ext), zero_tile)
    residual_block(vB, fine_add, gE, sE, 0)

    in1 = slice(ROWS_PAD, ROWS_PAD + ext1)

    def halved():
        pairs = get_strips(fine_add, pl.ds(0, ext1, 2)) + get_strips(fine_add, pl.ds(1, ext1, 2))
        return 0.25 * exact_dot(pairs, down0[...])

    g1[in1, :] = halved()
    put_strips(fine_add, slice(0, ext), sE[...])
    s1[in1, :] = halved()
    w1[in1, :] = weight(s1[in1, :], ROWS_PAD - base1, half_rows, cols // 2, half // 2, 1)
    a1[in1, :] = w1[in1, :] * g1[in1, :]
    sweep_block(a1, b1, g1, w1, 1)
    residual_block(b1, r1, g1, s1, 1)
    rbuf[1, me] = pack_level2(r1)
    gather_start(1)

    block = (lane_e[0:8] // 16)

    def unpack(turn, target):
        for x in range(gx_count):
            for u in range(gy_count // 8):
                for tl in range(2):
                    tiles = [rbuf[turn, x * gy_count + u * 8 + g, tl * 8 : tl * 8 + 8, :] for g in range(8)]
                    for bit in (1, 2, 4):
                        keep = (block & bit) == 0
                        fresh = list(tiles)
                        for g in range(8):
                            if g & bit == 0:
                                lo, hi = tiles[g], tiles[g | bit]
                                fresh[g] = jnp.where(keep, lo, pltpu.roll(hi, 16 * bit, 1))
                                fresh[g | bit] = jnp.where(keep, pltpu.roll(lo, lanes - 16 * bit, 1), hi)
                        tiles = fresh
                    for b in range(8):
                        t, r = (b // 4) * 2 + tl, b % 4
                        target[t * 4 + r, 8 * x : 8 * x + 8, u * lanes : (u + 1) * lanes] = tiles[b]

    lane_q = iota((p_count, q_count), 1)
    rows_q = slice(8, 8 + p_count)

    def sides(v, n, t, r):
        mid = v[t * n + r, rows_q, :]
        if t > 0:
            north = v[(t - 1) * n + r, rows_q, :]
        else:
            north = v[(n - 1) * n + r, 7 : 7 + p_count, :]
        if t < n - 1:
            south = v[(t + 1) * n + r, rows_q, :]
        else:
            south = v[r, 9 : 9 + p_count, :]
        if r > 0:
            west = v[t * n + r - 1, rows_q, :]
        else:
            west = jnp.where(lane_q == 0, 0.0, pltpu.roll(v[t * n + n - 1, rows_q, :], 1, 1))
        if r < n - 1:
            east = v[t * n + r + 1, rows_q, :]
        else:
            east = jnp.where(
                lane_q == q_count - 1, 0.0, pltpu.roll(v[t * n, rows_q, :], q_count - 1, 1)
            )
        return mid, (north + south) + (west + east)

    level_refs = {2: (s2, w2, g2, a2, b2, 4), 3: (s3, w3, g3, a3, b3, 2), 4: (s4, w4, g4, a4, b4, 1)}

    def sweep(level, v, out):
        s, w, g, _, _, n = level_refs[level]
        for t in range(n):
            for r in range(n):
                i = t * n + r
                mid, beside = sides(v, n, t, r)
                out[i, rows_q, :] = (1.0 - DAMPING) * mid + w[i] * (g[i] + 4.0 ** (-level) * beside)

    def first_sweep(level, out):
        s, w, g, _, _, n = level_refs[level]
        for i in range(n * n):
            out[i, rows_q, :] = w[i] * g[i]

    def restricted(level, v):
        s, w, g, _, _, n = level_refs[level]
        coarse_g = level_refs[level + 1][2]
        for t in range(n // 2):
            for r in range(n // 2):
                sums = None
                for dt in range(2):
                    for dr in range(2):
                        i = (2 * t + dt) * n + 2 * r + dr
                        mid, beside = sides(v, n, 2 * t + dt, 2 * r + dr)
                        left = g[i] - (4.0 ** (-level) * (4.0 * mid - beside) + s[i] * mid)
                        sums = left if sums is None else sums + left
                coarse_g[t * (n // 2) + r] = 0.25 * sums

    def correct(level, v, e):
        n = level_refs[level][5]
        for t in range(n):
            for r in range(n):
                i = t * n + r
                v[i, rows_q, :] = v[i, rows_q, :] + e[(t // 2) * (n // 2) + r // 2, rows_q, :]

    def prepare(level):
        s, w, _, _, _, n = level_refs[level]
        for i in range(n * n):
            w[i] = DAMPING / (4.0 ** (1 - level) + s[i])
        if level < 4:
            coarse_s = level_refs[level + 1][0]
            m = n // 2
            for t in range(m):
                for r in range(m):
                    i = 2 * t * n + 2 * r
                    coarse_s[t * m + r] = 0.25 * ((s[i] + s[i + n]) + (s[i + 1] + s[i + n + 1]))

    def total_of(x):
        return jnp.sum(jnp.sum(x, axis=0, keepdims=True), axis=1, keepdims=True)

    gather_wait(0)
    unpack(0, s2)
    for level in (2, 3, 4):
        prepare(level)
    row_q = iota((p_count, q_count), 0)
    edges = jnp.where(row_q == 0, 1.0, 0.0) + jnp.where(row_q == p_count - 1, 1.0, 0.0)
    edges = edges + jnp.where(lane_q == 0, 1.0, 0.0) + jnp.where(lane_q == q_count - 1, 1.0, 0.0)
    per_unit = 1.0 / total_of(4.0 ** (-4) * edges + s4[0])

    def coarse(v, from_zero):
        if from_zero:
            shifted = jnp.zeros((p_count, q_count), F32) + total_of(g4[0]) * per_unit
        else:
            mid, beside = sides(v, 1, 0, 0)
            left = g4[0] - (4.0 ** (-4) * (4.0 * mid - beside) + s4[0] * mid)
            shifted = mid + total_of(left) * per_unit
        now, later = a4, b4
        now[0, rows_q, :] = shifted
        for _ in range(COARSE_SWEEPS):
            sweep(4, now, later)
            now, later = later, now
        return now

    def vcycle(level, v):
        if level == 4:
            return coarse(v, v is None)
        _, _, _, a, b, n = level_refs[level]
        if v is None:
            first_sweep(level, a)
            sweep(level, a, b)
            now, later = b, a
        else:
            later = b if v is a else a
            sweep(level, v, later)
            sweep(level, later, v)
            now = v
        restricted(level, now)
        correct(level, now, vcycle(level + 1, None))
        sweep(level, now, later)
        sweep(level, later, now)
        return now

    def fcycle(level):
        if level == 4:
            return coarse(None, True)
        _, _, _, a, b, n = level_refs[level]
        first_sweep(level, a)
        sweep(level, a, b)
        restricted(level, b)
        e = fcycle(level + 1)
        e = vcycle(level + 1, e)
        correct(level, b, e)
        sweep(level, b, a)
        sweep(level, a, b)
        return b

    def add_level2(e, v):
        for t in range(4):
            tiles = [e[t * 4 + r, pl.ds(pl.multiple_of(gx * 8, 8), 24), :] for r in range(4)]
            picked[t] = exact_dot(jnp.concatenate(tiles, 1), spread[...])
        for t in range(4):
            for a in range(2):
                at = pl.ds(ROWS_PAD + 2 * t + a, ext1 // 8, 8)
                put_strips(r1, at, picked[t, 6 : 6 + ext1 // 8, :])
        v[in1, :] = v[in1, :] + get_strips(r1, in1)

    gather_wait(1)
    unpack(1, g2)
    e = fcycle(2)
    e = vcycle(2, e)
    add_level2(e, b1)
    sweep_block(b1, a1, g1, w1, 1)
    sweep_block(a1, b1, g1, w1, 1)
    sweep_block(b1, a1, g1, w1, 1)
    sweep_block(a1, b1, g1, w1, 1)
    residual_block(b1, r1, g1, s1, 1)
    rbuf[2, me] = pack_level2(r1)
    gather_start(2)
    gather_wait(2)
    unpack(2, g2)
    add_level2(vcycle(2, None), b1)
    sweep_block(b1, a1, g1, w1, 1)
    sweep_block(a1, b1, g1, w1, 1)
    raised = exact_dot(b1[in1, :], up0[...])
    put_strips(fine_add, pl.ds(0, ext1, 2), raised)
    put_strips(fine_add, pl.ds(1, ext1, 2), raised)
    for lo in range(ROWS_PAD, ext - ROWS_PAD, 8):
        at = slice(lo, lo + 8)
        vB[at, :] = vB[at, :] + get_strips(fine_add, at)
    sweep_block(vB, vA, gE, wE, 0)
    sweep_block(vA, vB, gE, wE, 0)
    for lo in range(0, rows, 8):
        mid, beside = around(vB, base + lo, 8)
        at = slice(base + lo, base + lo + 8)
        left = gE[at, :] - ((4.0 * mid - beside) + sE[at, :] * mid)
        out_ref[0, lo : lo + 8, :] = mid[:, 0:cols]
        out_ref[1, lo : lo + 8, :] = left[:, 0:cols]

    for n, (dx, dy, source, target) in enumerate(sends):
        @pl.when(inside(dx, dy))
        def _():
            halo_copy(n, dx, dy, source, target).wait_send()
    for turn in range(3):
        gather_sent(turn)


def solution(mesh):
    gx_count, gy_count = mesh.shape["gx"], mesh.shape["gy"]
    total = gx_count * gy_count

    def body(right_side, shift):
        rows, cols = right_side.shape
        assert cols == 256 and rows % 64 == 0 and gy_count % 8 == 0
        ext, width = rows + 2 * (HALO + ROWS_PAD), cols + 128
        ext1, width1 = ext // 2 + 2 * ROWS_PAD, 256
        p, q = rows // 16 * gx_count, cols // 16 * gy_count
        V = pltpu.VMEM
        big = [V((ext, width), F32)] * 5 + [V((width // 128, ext, 128), F32)]
        one = [V((ext1, width1), F32)] * 5 + [V((width1 // 128, ext1, 128), F32)]
        levels = []
        for n in (16, 4, 1):
            levels += [V((n, p, q), F32)] * 3 + [V((n, p + 16, q), F32)] * 2
        scratch = (
            big + one
            + [V((rows, 128), F32)] * 2 + [V((ext, 128), F32)] * 2
            + [V((width, width1), BF16), V((width1, width), BF16), V((width1, 128), BF16), V((4 * q, width1), BF16)]
            + [V((3, total, 16, 128), F32)]
            + levels
            + [V((4, 24, width1), F32)]
            + [
                pltpu.SemaphoreType.DMA((10,)), pltpu.SemaphoreType.DMA((10,)),
                pltpu.SemaphoreType.DMA((3, total)), pltpu.SemaphoreType.DMA((3, total)),
            ]
        )
        out = jax.ShapeDtypeStruct((2,) + right_side.shape, F32)
        both = pl.pallas_call(
            functools.partial(kernel, gx_count, gy_count),
            out_shape=out,
            in_specs=[pl.BlockSpec(memory_space=pltpu.VMEM)] * 2,
            out_specs=pl.BlockSpec(memory_space=pltpu.VMEM),
            scratch_shapes=scratch,
            compiler_params=pltpu.CompilerParams(
                collective_id=0, has_side_effects=True, vmem_limit_bytes=60 * 1024 * 1024
            ),
        )(right_side, shift)
        return both[0], both[1]

    spec = P("gx", "gy")
    return jax.shard_map(body, mesh=mesh, in_specs=(spec, spec), out_specs=(spec, spec), check_vma=False)
```
